32 devices in a mesh: wide: 16 (over z, x, core), blk: 2 (over y).
Axes of the slice: x: 2, y: 2, z: 4, core: 2. Of those that a mesh axis runs over, the one named last changes fastest.
Arguments:
- density: float32 [128, 49152], P(None, ('wide', 'blk')), may hold values from -6 to 6
- green_table: float32 [128, 384, 384], P(('wide', 'blk')), may hold values from -0.109375 to 0.109375
- corrections: float32 [384, 384, 384], P(('wide', 'blk')), may hold values from -0.3125 to 0.3125
- interp_index: int32 [128, 8], P(('wide', 'blk')), may hold values from 0 to 2
- interp_frac: float32 [128, 8], P(('wide', 'blk')), may hold values from 0 to 1
- pairs: int32 [384, 2], P(('wide', 'blk')), may hold values from 0 to 63, as said below
- counts: int32 [32], P(('wide', 'blk')), may hold values from 10 to 12, as said below
Outputs:
- image: float32 [128, 49152], P(None, ('wide', 'blk'))
The draws below stay inside these ranges and needn't reach their ends.
Inputs may be any that keep to these rules, and one draw needn't show every extreme that they name: `pairs`: row i belongs to device i // 12; column 0 is a receiver block 0 .. 3 of that device, column 1 a source block peer * 4 + j with peer a wide index and j < 4; the 12 slots of one device name 12 different peers. `counts`: entry d is the number of leading slots of device d in use; some device uses all 12.
All inputs are finite; a program needn't handle non-finite values.
Results may differ from the reference program's by a relative error of at most 0.0003.
Values sent between devices are 32-bit elements; how exact they have to be, the bound alone decides.
A program may use at most 320 MiB of HBM per device.

```python
import jax
import jax.numpy as jnp
from jax import lax

NRHS = 128
RB = 4
BLK = 384
TBL = 4
MAXCOR = 12
CYCLE = 8
NBLOCKS = 128
DOFS = 49152
TABLES = 128
CORRS = 384
N_WIDE = 16
N_BLK = 2


def pattern_draw(key):
    base_key = jax.random.fold_in(key, 11)
    key_perm, key_rows, key_inner, key_base, key_heavy, key_forced = jax.random.split(base_key, 6)
    dev_total = N_WIDE * N_BLK
    perm_keys = jax.random.split(key_perm, dev_total)
    peer_sets = jax.vmap(lambda one_key: jax.random.permutation(one_key, N_WIDE)[:MAXCOR])(perm_keys)
    row_pick = jax.random.randint(key_rows, (dev_total, MAXCOR), 0, RB)
    inner_pick = jax.random.randint(key_inner, (dev_total, MAXCOR), 0, RB)
    pair_rows = jnp.stack([row_pick, peer_sets * RB + inner_pick], axis=-1).reshape(dev_total * MAXCOR, 2).astype(jnp.int32)
    base_count = jax.random.randint(key_base, (dev_total,), MAXCOR * 5 // 6, MAXCOR + 1)
    heavy = jax.random.randint(key_heavy, (dev_total,), 0, 8) == 0
    forced = jax.random.randint(key_forced, (), 0, dev_total)
    chosen = heavy | (jnp.arange(dev_total) == forced)
    count_rows = jnp.where(chosen, MAXCOR, base_count).astype(jnp.int32)
    return (pair_rows, count_rows)


def draw_pairs(key, part):
    return pattern_draw(key)[0]


def draw_counts(key, part):
    return pattern_draw(key)[1]


def touch_ends(array, stream_key, low, largest):
    index_at = [jax.random.randint(jax.random.fold_in(stream_key, axis), (), 0, length) for axis, length in enumerate(array.shape)]
    widest = array.shape.index(max(array.shape))
    neighbour = index_at[:widest] + [(index_at[widest] + 1) % array.shape[widest]] + index_at[widest + 1:]
    return array.at[tuple(index_at)].set(low).at[tuple(neighbour)].set(largest)


def block_scale(stream_key, shape, cuts, least, top_value):
    loudness = 1.0
    for dim, parts in cuts:
        steps = jax.random.uniform(jax.random.fold_in(jax.random.fold_in(stream_key, 6), dim), (parts,), jnp.float32, least / len(cuts), top_value / len(cuts))
        loudness = loudness * jnp.repeat(jnp.exp(steps), shape[dim] // parts).reshape((-1,) + (1,) * (len(shape) - 1 - dim))
    return loudness


def noise(own_key, extent, deviation, most, pieces=(), kind=jnp.bfloat16):
    result = jax.random.normal(own_key, extent, jnp.float32) * deviation
    if len(pieces) > 0:
        result = block_scale(own_key, extent, pieces, -0.22, 0.18) * result
    return jnp.clip(result, min=-most, max=most).astype(kind)


def setup_inputs(seed: int = 0) -> dict:
    splits = jax.random.split(jax.random.key(seed), 8)
    return {
        "density": noise(splits[0], (NRHS, DOFS), 1.0, 6.0, ((1, 32),), jnp.float32),
        "green_table": noise(splits[1], (TABLES, BLK, BLK), (CYCLE * BLK) ** -0.5, 0.109375, ((0, 32),), jnp.float32),
        "corrections": noise(splits[2], (CORRS, BLK, BLK), BLK ** -0.5, 0.3125, ((0, 32),), jnp.float32),
        "interp_index": touch_ends(jax.random.randint(splits[3], (NBLOCKS, CYCLE), 0, TBL - 1), jax.random.fold_in(splits[3], 1), 0, (TBL - 1) - 1).astype(jnp.int32),
        "interp_frac": jnp.clip(1.0 * jax.random.uniform(splits[4], (NBLOCKS, CYCLE), jnp.float32) ** block_scale(splits[4], (NBLOCKS, CYCLE), ((0, 32),), -0.2, 0.2), 0.0, 1.0),
        "pairs": draw_pairs(jax.random.fold_in(splits[7], 71), 0),
        "counts": draw_counts(jax.random.fold_in(splits[7], 71), 0),
    }


def interp_weights(index_rows, frac_rows):
    levels = jnp.arange(TBL, dtype=jnp.int32)
    lower = (index_rows[..., None] == levels).astype(jnp.float32)
    upper = ((index_rows[..., None] + 1) == levels).astype(jnp.float32)
    return (1.0 - frac_rows)[..., None] * lower + frac_rows[..., None] * upper


def reference(density, green_table, corrections, interp_index, interp_frac, pairs, counts):
    exact = lax.Precision.HIGHEST
    dev_total = N_WIDE * N_BLK
    blocks_all = density.reshape(NRHS, N_WIDE, N_BLK, RB, BLK)
    tables = green_table.reshape(dev_total, TBL, BLK, BLK)
    index_all = interp_index.reshape(dev_total, RB, CYCLE)
    frac_all = interp_frac.reshape(dev_total, RB, CYCLE)
    corr_all = corrections.reshape(dev_total, MAXCOR, BLK, BLK)
    pair_all = pairs.reshape(dev_total, MAXCOR, 2)

    def one_device(carry, inputs):
        device, table_here, index_here, frac_here, corr_here, pair_here, used = inputs
        wide_at = device // N_BLK
        blk_at = device % N_BLK
        cycle_part = lax.dynamic_index_in_dim(blocks_all, wide_at, axis=1, keepdims=False)
        source = cycle_part.reshape(NRHS, CYCLE, BLK)
        weights = interp_weights(index_here, frac_here)
        products = jnp.einsum("kab,nsb->ksna", table_here, source, precision=exact)
        far_part = jnp.einsum("rsk,ksna->nra", weights, products, precision=exact)
        column = lax.dynamic_index_in_dim(blocks_all, blk_at, axis=2, keepdims=False)
        column = column.reshape(NRHS, N_WIDE * RB, BLK)
        picked = jnp.take(column, pair_here[:, 1], axis=1)
        near_each = jnp.einsum("kab,nkb->nka", corr_here, picked, precision=exact)
        is_used = jnp.arange(MAXCOR, dtype=jnp.int32) < used
        near_each = jnp.where(is_used[None, :, None], near_each, jnp.float32(0.0))
        placing = (pair_here[:, 0][:, None] == jnp.arange(RB, dtype=jnp.int32)[None, :]).astype(jnp.float32)
        near_part = jnp.einsum("kr,nka->nra", placing, near_each, precision=exact)
        own_part = lax.dynamic_index_in_dim(cycle_part, blk_at, axis=1, keepdims=False)
        return carry, 0.5 * own_part + far_part + near_part

    _, outputs = lax.scan(one_device, jnp.zeros((), jnp.float32),
                          (jnp.arange(dev_total, dtype=jnp.int32), tables, index_all, frac_all, corr_all, pair_all, counts))
    return jnp.transpose(outputs, (1, 0, 2, 3)).reshape(NRHS, DOFS)
```

```python
import functools

import jax
import jax.numpy as jnp
from jax import lax
from jax.experimental import pallas as pl
from jax.experimental.pallas import tpu as pltpu
from jax.sharding import PartitionSpec as P

MESH = pl.DeviceIdType.MESH
CHUNKS = 8
NT = (((1,), (1,)), ((), ()))


def split(value):
    high = value.astype(jnp.bfloat16)
    low = (value - high.astype(jnp.float32)).astype(jnp.bfloat16)
    return high, low


def product(value, high_t, low_t):
    rows = value.shape[0]
    high, low = split(value)
    both = lax.dot_general(
        jnp.concatenate([high, low], axis=0), high_t, NT, preferred_element_type=jnp.float32
    )
    rest = lax.dot_general(high, low_t, NT, preferred_element_type=jnp.float32)
    return both[:rows] + both[rows:] + rest


def kernel(
    depth, parts,
    pairs_hbm, counts, index_hbm, frac_hbm, density_hbm, green_hbm, corr_hbm,
    out,
    pairs, index, frac,
    held, fsend, frecv, cycle, corr, corr_high, corr_low, green, green_high, green_low,
    request, asked, row_of, slot_of, mixed,
    load_sem, own_sem, z_send, z_recv, f_send, f_recv, b_send, b_recv, q_send, q_recv,
):
    wide = lax.axis_index("wide")
    blk = lax.axis_index("blk")
    core = lax.rem(wide, 2)
    side = lax.rem(lax.div(wide, 2), 2)
    z = lax.div(wide, 4)
    peers = 4 * depth
    rhs, local = density_hbm.shape
    density = cycle.at[blk]
    slots = corr.shape[0]
    levels = green.shape[0]
    block = corr.shape[1]
    rows = local // block
    step_rows = rhs // CHUNKS

    def place(o):
        at_side = 1 - side if o & 2 else side
        at_core = 1 - core if o & 1 else core
        return at_side * 2 + at_core

    def chunk(ch):
        return pl.ds(pl.multiple_of(ch * step_rows, step_rows), step_rows)

    def corr_load(j):
        return pltpu.make_async_copy(corr_hbm.at[j], corr.at[j], load_sem.at[j])

    def green_load(k):
        return pltpu.make_async_copy(green_hbm.at[k], green.at[k], load_sem.at[slots + k])

    def z_copy(d, s, ch, source=None):
        zz = z - s if d == 0 else z + s
        to = wide + 4 if d == 0 else wide - 4
        return pltpu.make_async_remote_copy(
            src_ref=(held.at[zz] if source is None else source).at[chunk(ch)],
            dst_ref=held.at[zz].at[chunk(ch)],
            send_sem=z_send.at[d, s],
            recv_sem=z_recv.at[d, s, ch],
            device_id={"wide": to},
            device_id_type=MESH,
        )

    def z_whole(d, s):
        zz = z - s if d == 0 else z + s
        return pltpu.make_async_remote_copy(
            src_ref=held.at[zz],
            dst_ref=held.at[zz],
            send_sem=z_send.at[d, s],
            recv_sem=z_recv.at[d, s, 0],
            device_id={"wide": wide},
            device_id_type=MESH,
        )

    def z_arrival(d, s, ch):
        zz = z - 1 - s if d == 0 else z + 1 + s
        return pltpu.make_async_remote_copy(
            src_ref=held.at[zz].at[chunk(ch)],
            dst_ref=held.at[zz].at[chunk(ch)],
            send_sem=z_send.at[d, s],
            recv_sem=z_recv.at[d, s, ch],
            device_id={"wide": wide},
            device_id_type=MESH,
        )

    def f_copy(zz, o, window):
        return pltpu.make_async_remote_copy(
            src_ref=fsend.at[zz, o - 1].at[window],
            dst_ref=frecv.at[zz, o - 1].at[window],
            send_sem=f_send.at[zz, o - 1],
            recv_sem=f_recv.at[zz, o - 1],
            device_id={"wide": z * 4 + place(o)},
            device_id_type=MESH,
        )

    def b_copy(t):
        return pltpu.make_async_remote_copy(
            src_ref=density_hbm,
            dst_ref=cycle.at[blk],
            send_sem=b_send.at[t - 1],
            recv_sem=b_recv.at[t - 1],
            device_id={"blk": lax.rem(blk + t, parts)},
            device_id_type=MESH,
        )

    def b_arrival(t):
        source = lax.rem(blk + parts - t, parts)
        return pltpu.make_async_remote_copy(
            src_ref=density_hbm,
            dst_ref=cycle.at[source],
            send_sem=b_send.at[t - 1],
            recv_sem=b_recv.at[t - 1],
            device_id={"blk": lax.rem(blk + t, parts)},
            device_id_type=MESH,
        )

    def q_copy(o):
        return pltpu.make_async_remote_copy(
            src_ref=request,
            dst_ref=asked.at[o - 1],
            send_sem=q_send.at[o - 1],
            recv_sem=q_recv.at[o - 1],
            device_id={"wide": z * 4 + place(o)},
            device_id_type=MESH,
        )

    def z_source(d, s):
        return z - 1 - s if d == 0 else z + 1 + s

    def z_exists(d, s):
        return z - 1 - s >= 0 if d == 0 else z + 1 + s <= depth - 1

    def z_onward(d):
        return z < depth - 1 if d == 0 else z > 0

    def pick(source, window, wanted):
        want = jnp.broadcast_to(wanted, (wanted.shape[0] * window.size, block))
        got = source[window, 0:block]
        for i in range(1, rows):
            got = jnp.where(want == i, source[window, i * block : (i + 1) * block], got)
        return got

    def forward(source, zz, ch):
        mine = zz * 4 + place(0)
        for o in (2, 3, 1):
            wanted = asked[o - 1, pl.ds(mine, 1), :]
            fsend[zz, o - 1, chunk(ch), :] = pick(source, chunk(ch), wanted)
            f_copy(zz, o, chunk(ch)).start()

    def near_one(value, peer):
        j = slot_of[peer]
        found = product(value, corr_high[j], corr_low[j])
        row = jnp.broadcast_to(row_of[pl.ds(peer, 1), :], (rhs, block))
        for r in range(rows):
            at = slice(r * block, (r + 1) * block)
            out[:, at] += jnp.where(row == r, found, 0.0)

    def near(source, zz):
        mine = zz * 4 + place(0)
        near_one(pick(source, pl.ds(0, rhs), request[pl.ds(mine, 1), :]), mine)
        for o in (1, 2, 3):
            f_copy(zz, o, pl.ds(0, rhs)).wait_recv()
            near_one(frecv[zz, o - 1], zz * 4 + place(o))

    def loop(count, body):
        lax.fori_loop(0, count, lambda i, c: (body(i), c)[1], 0)

    barrier = pltpu.get_barrier_semaphore()
    for d in range(2):
        @pl.when(z_onward(d))
        def _(d=d):
            pl.semaphore_signal(
                barrier, inc=1, device_id={"wide": wide + 4 if d == 0 else wide - 4}, device_id_type=MESH
            )
    for o in (1, 2, 3):
        pl.semaphore_signal(barrier, inc=1, device_id={"wide": z * 4 + place(o)}, device_id_type=MESH)
    for t in range(1, parts):
        pl.semaphore_signal(barrier, inc=1, device_id={"blk": lax.rem(blk + t, parts)}, device_id_type=MESH)

    ends = jnp.where(z < depth - 1, 1, 0) + jnp.where(z > 0, 1, 0)
    pl.semaphore_wait(barrier, 3 + parts - 1 + ends)

    def send_own(ch):
        for d in range(2):
            @pl.when(z_onward(d))
            def _(d=d):
                z_copy(d, 0, ch, density_hbm).start()

    loop(CHUNKS, send_own)
    for t in range(1, parts):
        b_copy(t).start()
    small = [
        pltpu.make_async_copy(source, target, own_sem.at[1 + i])
        for i, (source, target) in enumerate(
            ((pairs_hbm, pairs), (index_hbm, index), (frac_hbm, frac))
        )
    ]
    for copy in small:
        copy.start()
    own = pltpu.make_async_copy(density_hbm, density, own_sem.at[0])
    own.start()
    loop(levels, lambda k: green_load(k).start())
    loop(slots, lambda j: corr_load(j).start())
    for copy in small:
        copy.wait()

    peer_at = lax.broadcasted_iota(jnp.int32, (peers, block), 0)
    wanted = jnp.zeros((peers, block), jnp.int32)
    row = jnp.full((peers, block), -1, jnp.int32)
    used = counts[0]
    for j in range(slots):
        source = pairs[1, j]
        here = peer_at == lax.div(source, rows)
        wanted = jnp.where(here, lax.rem(source, rows), wanted)
        row = jnp.where(here, jnp.where(j < used, pairs[0, j], -1), row)
    request[...] = wanted
    row_of[...] = row

    def find_slot(p):
        found = jnp.int32(0)
        for j in range(slots):
            found = jnp.where(lax.div(pairs[1, j], rows) == p, j, found)
        slot_of[p] = found

    for o in (2, 3, 1):
        q_copy(o).start()
    loop(peers, find_slot)
    out[...] = jnp.zeros_like(out)
    own.wait()

    for o in (1, 2, 3):
        q_copy(o).wait_recv()
    loop(CHUNKS, lambda ch: forward(density, z, ch))

    def split_green(k):
        green_load(k).wait()
        green_high[k], green_low[k] = split(green[k])

    def split_corr(j):
        corr_load(j).wait()
        corr_high[j], corr_low[j] = split(corr[j])

    loop(levels, split_green)
    loop(slots, split_corr)

    def far_level(k):
        def mix(r):
            total = jnp.zeros((rhs, block), jnp.float32)

            def add(q, total):
                for i in range(rows):
                    s = q * rows + i
                    low = index[r, s]
                    f = frac[r, s]
                    zero = jnp.float32(0.0)
                    weight = jnp.where(low == k, 1.0 - f, zero) + jnp.where(low + 1 == k, f, zero)
                    total = total + weight * cycle[q, :, i * block : (i + 1) * block]
                return total

            mixed[pl.ds(pl.multiple_of(r * rhs, rhs), rhs), :] = lax.fori_loop(0, parts, add, total)

        loop(rows, mix)
        found = product(mixed[...], green_high[k], green_low[k])
        for r in range(rows):
            out[:, r * block : (r + 1) * block] += found[r * rhs : (r + 1) * rhs]

    def take(s):
        def one(ch):
            for d in range(2):
                @pl.when(z_exists(d, s))
                def _(d=d):
                    z_arrival(d, s, ch).wait_recv()

                    @pl.when(z_onward(d))
                    def _():
                        z_copy(d, s + 1, ch).start()

                    forward(held.at[z_source(d, s)], z_source(d, s), ch)

        loop(CHUNKS, one)

    def near_step(s):
        for d in range(2):
            @pl.when(z_exists(d, s))
            def _(d=d):
                near(held.at[z_source(d, s)], z_source(d, s))

    take(0)
    near(density, z)
    for t in range(1, parts):
        b_arrival(t).wait_recv()
    loop(levels, far_level)

    def later(s):
        take(s)
        near_step(s - 1)

    lax.fori_loop(1, depth - 1, lambda s, c: (later(s), c)[1], 0)
    near_step(depth - 2)

    def z_done(s):
        for d in range(2):
            zz = z - s if d == 0 else z + s
            there = zz >= 0 if d == 0 else zz <= depth - 1

            @pl.when(there)
            def _(d=d):
                @pl.when(z_onward(d))
                def _():
                    z_whole(d, s).wait_send()

    loop(depth - 1, z_done)

    def f_done(zz):
        for o in (1, 2, 3):
            f_copy(zz, o, pl.ds(0, rhs)).wait_send()

    loop(depth, f_done)
    for o in (1, 2, 3):
        q_copy(o).wait_send()
    for t in range(1, parts):
        b_copy(t).wait_send()


def capacity(depth, rows):
    return 5 * (depth - 1) * rows // 6 - 1


DIRECT = 2
UNROLL = 6
NN = (((1,), (0,)), ((), ()))


def product_nn(value, high, low):
    rows = value.shape[0]
    top, bottom = split(value)
    both = lax.dot_general(
        jnp.concatenate([top, bottom], axis=0), high, NN, preferred_element_type=jnp.float32
    )
    rest = lax.dot_general(top, low, NN, preferred_element_type=jnp.float32)
    return both[:rows] + both[rows:] + rest


def cuts(rhs):
    sizes = [rhs // 16] * 2 + [rhs // 8] * 5 + [rhs // 16] * 4
    return sizes, [sum(sizes[:i]) for i in range(len(sizes))]


def packed_kernel(
    depth, parts, block,
    pairs_hbm, counts, index_hbm, frac_hbm, density_hbm, green_hbm, corr_hbm,
    out, spill,
    pairs, index, frac, cycle, corr, corr_high, corr_low, green, green_high, green_low, mixed,
    want, asked, ends, at, ahead, chosen, picks, direct, line_at, other_at, row_of, flag, below, above, beside,
    load_sem, own_sem, z_send, z_recv, f_send, f_recv, b_send, b_recv, q_send, q_recv, e_send, e_recv, d_send, d_recv,
    flag_send, flag_recv, side_send, side_recv,
    *chunked,
):
    wide = lax.axis_index("wide")
    blk = lax.axis_index("blk")
    core = lax.rem(wide, 2)
    side = lax.rem(lax.div(wide, 2), 2)
    spot = side * 2 + core
    z = lax.div(wide, 4)
    peers = 4 * depth
    rhs, local = density_hbm.shape
    slots = corr.shape[0]
    levels = green.shape[0]
    rows = local // block
    sizes, starts = cuts(rhs)
    steps = len(sizes)
    mixed_steps = steps - DIRECT
    cand, taken, given, pack = (chunked[i * steps : (i + 1) * steps] for i in range(4))
    room = capacity(depth, rows)
    wanted_end = depth - 1
    candidates = wanted_end * rows

    near_way = jnp.where(2 * z < depth, 0, 1)
    far_way = 1 - near_way

    def rank(d):
        return jnp.where(d == 0, z, depth - 1 - z)

    def plane(d, t):
        return jnp.where(d == 0, t, depth - 1 - t)

    def base(d):
        return jnp.where(d == 0, 0, rows)

    def onward(d):
        return jnp.where(d == 0, wide + 4, wide - 4)

    def backward(d):
        return jnp.where(d == 0, wide - 4, wide + 4)

    near_rank, far_rank = rank(near_way), rank(far_way)

    def place(o):
        at_side = 1 - side if o & 2 else side
        at_core = 1 - core if o & 1 else core
        return at_side * 2 + at_core

    def remote(source, target, send, recv, device):
        return pltpu.make_async_remote_copy(
            src_ref=source, dst_ref=target, send_sem=send, recv_sem=recv,
            device_id=device, device_id_type=MESH,
        )

    def corr_load(j):
        return pltpu.make_async_copy(corr_hbm.at[j], corr.at[j], load_sem.at[j])

    def green_load(k):
        return pltpu.make_async_copy(green_hbm.at[k], green.at[k], load_sem.at[slots + k])

    def hop(d, t, ch):
        window = cand[ch].at[pl.ds(plane(d, t) * rows, rows)]
        return remote(window, window, z_send.at[d, t, ch], z_recv.at[d, t, ch], {"wide": onward(d)})

    def first_hop(d, ch):
        return remote(
            cand[ch].at[pl.ds(z * rows, 1)],
            cand[ch].at[pl.ds(base(d) + candidates - 1, 1)],
            z_send.at[d, depth - 2, ch], z_recv.at[d, depth - 2, ch], {"wide": onward(d)},
        )

    def last_hop(d, ch):
        return remote(
            pack[ch], cand[ch].at[pl.ds(base(d), room)],
            z_send.at[d, depth - 1, ch], z_recv.at[d, depth - 1, ch], {"wide": onward(d)},
        )

    def d_copy(o, ch):
        there = jnp.where(far_way == 0, depth - 1, 0) * 4 + place(o)
        return remote(
            pack[ch].at[pl.ds(o * wanted_end, wanted_end)],
            taken[ch].at[pl.ds(o * depth + jnp.where(far_way == 0, 0, 1), wanted_end)],
            d_send.at[o, ch - mixed_steps], d_recv.at[o, ch - mixed_steps], {"wide": there},
        )

    def own_copy(o, ch):
        window = pl.ds(o * depth + z, 1)
        return remote(
            given[ch].at[window], taken[ch].at[window],
            f_send.at[o - 1, ch], f_recv.at[o - 1, ch], {"wide": z * 4 + place(o)},
        )

    def f_copy(o, ch):
        window = pl.ds(o * depth, depth)
        return remote(
            given[ch].at[window], taken[ch].at[window],
            f_send.at[o - 1, ch], f_recv.at[o - 1, ch], {"wide": z * 4 + place(o)},
        )

    def b_copy(t):
        return remote(
            density_hbm, cycle.at[blk], b_send.at[t - 1], b_recv.at[t - 1],
            {"blk": lax.rem(blk + t, parts)},
        )

    def b_arrival(t):
        return remote(
            density_hbm, cycle.at[lax.rem(blk + parts - t, parts)], b_send.at[t - 1], b_recv.at[t - 1],
            {"blk": lax.rem(blk + t, parts)},
        )

    def q_copy(o):
        return remote(want, asked.at[o - 1], q_send.at[o - 1], q_recv.at[o - 1], {"wide": z * 4 + place(o)})

    def e_copy(q):
        goal = jnp.where(z == 0, 4, (depth - 2) * 4) + q
        return remote(want, ends.at[spot], e_send.at[q], e_recv.at[spot], {"wide": goal})

    def e_arrival(q):
        return remote(want, ends.at[q], e_send.at[q], e_recv.at[q], {"wide": wide})

    def flag_copy(d):
        return remote(flag.at[d], below if d == 0 else above, flag_send.at[d], flag_recv.at[d], {"wide": onward(d)})

    def side_copy(t):
        return remote(
            flag.at[2], beside.at[t - 1], side_send.at[t - 1], side_recv.at[t - 1],
            {"blk": lax.rem(blk + t, parts)},
        )

    def loop(count, body, unroll=1):
        lax.fori_loop(0, count, lambda i, c: (body(i), c)[1], 0, unroll=unroll)

    own = pltpu.make_async_copy(density_hbm, cycle.at[blk], own_sem.at[0])
    small = [
        pltpu.make_async_copy(source, target, own_sem.at[1 + i])
        for i, (source, target) in enumerate(
            ((pairs_hbm, pairs), (index_hbm, index), (frac_hbm, frac))
        )
    ]
    for copy in small:
        copy.start()
    own.start()
    below[0] = 0
    above[0] = 0
    barrier = pltpu.get_barrier_semaphore()

    def greet(device):
        pl.semaphore_signal(barrier, inc=1, device_id=device, device_id_type=MESH)

    end = jnp.logical_or(z == 0, z == depth - 1)
    for d in range(2):
        @pl.when(rank(d) < depth - 1)
        def _(d=d):
            greet({"wide": onward(d)})
    for o in (1, 2, 3):
        greet({"wide": z * 4 + place(o)})

    @pl.when(far_rank == depth - 2)
    def _():
        for o in (1, 2, 3):
            greet({"wide": jnp.where(far_way == 0, (depth - 1) * 4, 0) + place(o)})

    @pl.when(end)
    def _():
        for o in (1, 2, 3):
            greet({"wide": jnp.where(z == 0, 4, (depth - 2) * 4) + place(o)})

    for t in range(1, parts):
        greet({"blk": lax.rem(blk + t, parts)})
    loop(levels, lambda k: green_load(k).start())
    loop(slots, lambda j: corr_load(j).start())

    for copy in small:
        copy.wait()
    used = counts[0]
    peer = [jnp.where(j < used, lax.div(pairs[1, j], rows), -1) for j in range(slots)]
    inner = [lax.rem(pairs[1, j], rows) for j in range(slots)]

    def find(p):
        got = jnp.int32(-1)
        for j in range(slots):
            got = jnp.where(peer[j] == p, inner[j], got)
        want[p] = got

    loop(peers, find)
    own.wait()
    for ch in range(steps):
        for b in range(rows):
            cand[ch][z * rows + b] = cycle[
                blk, starts[ch] : starts[ch] + sizes[ch], b * block : (b + 1) * block
            ]
    ends_here = jnp.where(end, 3 + 1, jnp.where(far_rank == depth - 2, 3 + 2, 2))
    pl.semaphore_wait(barrier, 3 + parts - 1 + ends_here)

    @pl.when(end)
    def _():
        for q in range(4):
            e_copy(q).start()

    for o in (2, 3, 1):
        q_copy(o).start()

    def start_own(d, r, ch):
        hop(d, r, ch).start()

    @pl.when(far_rank == depth - 2)
    def _():
        first_hop(far_way, 0).start()

    for ch in range(steps):
        if ch < 1:
            start_own(near_way, near_rank, ch)
        else:
            @pl.when(near_rank == 0)
            def _(ch=ch):
                start_own(near_way, near_rank, ch)
        if ch < 1:
            @pl.when(far_rank < depth - 2)
            def _(ch=ch):
                start_own(far_way, far_rank, ch)
        if 0 < ch < mixed_steps:
            @pl.when(far_rank == depth - 2)
            def _(ch=ch):
                first_hop(far_way, ch).start()
    for t in range(1, parts):
        b_copy(t).start()

    def split_green(k):
        green_load(k).wait()
        green_high[k], green_low[k] = split(green[k].T)

    def split_corr(j):
        corr_load(j).wait()
        corr_high[j], corr_low[j] = split(corr[j].T)

    loop(levels, split_green)
    loop(slots // 2, split_corr)

    def needed(asker, d, line):
        found = []
        for t in range(wanted_end):
            asks = [asker(q, plane(d, t) * 4 + line) for q in range(4)]
            for b in range(rows):
                if (t, b) == (wanted_end - 1, 0):
                    found.append(None)
                    continue
                hit = asks[0] == b
                for ask in asks[1:]:
                    hit = jnp.logical_or(hit, ask == b)
                found.append(hit)
        return found

    @pl.when(far_rank == depth - 2)
    def _():
        for q in range(4):
            e_arrival(q).wait_recv()
        hits = needed(lambda q, p: ends[q, p], far_way, spot)
        later = jnp.int32(candidates)
        ahead[candidates] = later
        for i in reversed(range(candidates)):
            if hits[i] is not None:
                later = jnp.where(hits[i], i, later)
            ahead[i] = later
        now = ahead[0]
        for s in range(room):
            i = jnp.minimum(now, candidates - 1)
            chosen[s] = plane(far_way, lax.div(i, rows)) * rows + lax.rem(i, rows)
            now = ahead[jnp.minimum(now + 1, candidates)]
        lowest = jnp.where(far_way == 0, 0, 1)
        for o in range(4):
            for i in range(wanted_end):
                ask = ends[place(o), (lowest + i) * 4 + spot]
                direct[o * wanted_end + i] = (lowest + i) * rows + jnp.maximum(ask, 0)

    for o in (1, 2, 3):
        q_copy(o).wait_recv()
    for i in range(depth * rows):
        at[i] = i

    @pl.when(far_rank == depth - 1)
    def _():
        def asker(q, p):
            return want[p] if q == 0 else asked[q - 1, p]

        place_at = jnp.int32(0)
        hits = needed(asker, far_way, spot)
        for t in range(wanted_end):
            for b in range(rows):
                hit = hits[t * rows + b]
                if hit is None:
                    to = candidates - 1
                else:
                    to = jnp.minimum(place_at, room - 1)
                    place_at = place_at + jnp.where(hit, 1, 0)
                at[plane(far_way, t) * rows + b] = base(far_way) + to

    for o in range(4):
        for zz in range(depth):
            ask = want[zz * 4 + spot] if o == 0 else asked[o - 1, zz * 4 + spot]
            picks[o * depth + zz] = at[zz * rows + jnp.maximum(ask, 0)]

    def take(d, r, ch):
        for t in range(depth - 2):
            @pl.when(t < r)
            def _(t=t):
                hop(d, t, ch).wait_recv()

    def pass_on(d, r, ch):
        for t in range(depth - 3):
            @pl.when(t < r)
            def _(t=t):
                hop(d, t, ch).start()
        if ch + 1 < steps:
            start_own(d, r, ch + 1)

    def near_side(ch):
        @pl.when(near_rank > 0)
        def _():
            take(near_way, near_rank, ch)
            pass_on(near_way, near_rank, ch)

    def far_side(ch):
        @pl.when(far_rank < depth - 1)
        def _():
            take(far_way, far_rank, ch)

        if depth > 4:
            @pl.when(far_rank < depth - 2)
            def _():
                pass_on(far_way, far_rank, ch)

        @pl.when(far_rank == depth - 2)
        def _():
            if ch < mixed_steps:
                def fill(s):
                    pack[ch][s] = cand[ch][chosen[s]]

                loop(room, fill, True)
                last_hop(far_way, ch).start()
            else:
                for o in (2, 3, 0, 1):
                    def fill(i, o=o):
                        pack[ch][o * wanted_end + i] = cand[ch][direct[o * wanted_end + i]]

                    loop(wanted_end, fill, True)
                    d_copy(o, ch).start()

        if ch < mixed_steps:
            @pl.when(far_rank == depth - 1)
            def _():
                first_hop(far_way, ch).wait_recv()
                last_hop(far_way, ch).wait_recv()

    def forward_all(ch):
        for o in (2, 3, 1):
            def fill(zz, o=o):
                i = o * depth + zz
                given[ch][i] = cand[ch][picks[i]]

            loop(depth, fill, True)
            f_copy(o, ch).start()

    def forward(ch):
        if ch < mixed_steps:
            forward_all(ch)
            return

        @pl.when(jnp.logical_not(end))
        def _():
            forward_all(ch)

    def forward_own():
        @pl.when(end)
        def _():
            for ch in range(mixed_steps, steps):
                taken[ch][z] = cand[ch][picks[z]]
                for o in (2, 3, 1):
                    given[ch][o * depth + z] = cand[ch][picks[o * depth + z]]
                    own_copy(o, ch).start()

    def retire(ch):
        hop(near_way, near_rank, ch).wait_send()
        for t in range(depth - 3):
            @pl.when(t < near_rank)
            def _(t=t):
                hop(near_way, t, ch).wait_send()

        if depth > 4:
            @pl.when(far_rank < depth - 2)
            def _():
                for t in range(depth - 3):
                    @pl.when(t < far_rank)
                    def _(t=t):
                        hop(far_way, t, ch).wait_send()

                hop(far_way, far_rank, ch).wait_send()

        @pl.when(far_rank == depth - 2)
        def _():
            if ch < mixed_steps:
                first_hop(far_way, ch).wait_send()
                last_hop(far_way, ch).wait_send()
            else:
                for o in range(4):
                    d_copy(o, ch).wait_send()

        if ch < mixed_steps:
            for o in (1, 2, 3):
                f_copy(o, ch).wait_send()
        else:
            @pl.when(end)
            def _():
                for o in (1, 2, 3):
                    own_copy(o, ch).wait_send()

            @pl.when(jnp.logical_not(end))
            def _():
                for o in (1, 2, 3):
                    f_copy(o, ch).wait_send()

    def where_slots():
        for j in range(slots):
            p = lax.div(pairs[1, j], rows)
            zz, q = lax.div(p, 4), lax.rem(p, 4)
            flip_side = jnp.where(lax.div(q, 2) == side, 0, 2)
            flip_core = jnp.where(lax.rem(q, 2) == core, 0, 1)
            o = flip_side + flip_core
            line_at[j] = jnp.where(o == 0, at[zz * rows + lax.rem(pairs[1, j], rows)], -1)
            other_at[j] = o * depth + zz
            row_of[j] = jnp.where(j < used, pairs[0, j], -1)

    def near(group, j):
        here = line_at[j]
        there = other_at[j]
        mine = jnp.maximum(here, 0)
        low, high = starts[group[0]], starts[group[-1]] + sizes[group[-1]]
        parts_of = []
        for ch in group:
            from_line = here if ch < mixed_steps else jnp.where(end, -1, here)
            is_line = jnp.broadcast_to(from_line, (sizes[ch], block)) >= 0
            parts_of.append(jnp.where(is_line, cand[ch][mine], taken[ch][there]))
        found = product_nn(jnp.concatenate(parts_of, axis=0), corr_high[j], corr_low[j])
        row = jnp.broadcast_to(row_of[j], (high - low, block))
        for r in range(rows):
            out[low:high, r * block : (r + 1) * block] += jnp.where(row == r, found, 0.0)

    def ready(group):
        for ch in group:
            if ch < mixed_steps:
                for o in (1, 2, 3):
                    f_copy(o, ch).wait_recv()
            else:
                @pl.when(end)
                def _(ch=ch):
                    for o in (1, 2, 3):
                        own_copy(o, ch).wait_recv()
                    for o in range(4):
                        d_copy(o, ch).wait_recv()

                @pl.when(jnp.logical_not(end))
                def _(ch=ch):
                    for o in (1, 2, 3):
                        f_copy(o, ch).wait_recv()

    def far_level(k):
        def mix(r):
            total = jnp.zeros((rhs, block), jnp.float32)

            def add(q, total):
                for i in range(rows):
                    s = q * rows + i
                    low = index[r, s]
                    f = frac[r, s]
                    zero = jnp.float32(0.0)
                    weight = jnp.where(low == k, 1.0 - f, zero) + jnp.where(low + 1 == k, f, zero)
                    total = total + weight * cycle[q, :, i * block : (i + 1) * block]
                return total

            mixed[pl.ds(pl.multiple_of(r * rhs, rhs), rhs), :] = lax.fori_loop(0, parts, add, total)

        loop(rows, mix)
        found = product_nn(mixed[...], green_high[k], green_low[k])
        for r in range(rows):
            out[:, r * block : (r + 1) * block] += found[r * rhs : (r + 1) * rhs]

    def far(low, high):
        lax.fori_loop(low, high, lambda k, c: (far_level(k), c)[1], 0)

    def judge():
        flag[0, 0] = 0

        @pl.when(far_rank == depth - 2)
        def _():
            def line(q, worst):
                total = jnp.int32(0)
                for hit in needed(lambda e, p: ends[e, p], far_way, q):
                    if hit is not None:
                        total = total + jnp.where(hit, 1, 0)
                return jnp.maximum(worst, total)

            worst = lax.fori_loop(0, 4, line, jnp.int32(0))
            flag[0, 0] = jnp.where(worst > room, 1, 0)

        flag[1, 0] = flag[0, 0]
        flag[2, 0] = flag[0, 0]

    def relay_flag(i):
        for d in range(2):
            @pl.when(rank(d) == i)
            def _(d=d):
                if i > 0:
                    flag_copy(d).wait_recv()
                    got = below if d == 0 else above
                    flag[d, 0] = jnp.maximum(flag[d, 0], got[0])
                    flag[2, 0] = jnp.maximum(flag[2, 0], got[0])
                if i < depth - 1:
                    flag_copy(d).start()

    def share_flag():
        for t in range(1, parts):
            side_copy(t).start()

    def close_flag():
        worst = flag[2, 0]
        for t in range(1, parts):
            side_copy(t).wait_recv()
            worst = jnp.maximum(worst, beside[t - 1, 0])
        spill[0] = worst

    early, late = list(range(steps - 4)), list(range(steps - 4, steps))
    near_side(0)
    for c in range(steps):
        if c + 1 < steps:
            near_side(c + 1)
        far_side(c)
        forward(c)
        if c >= 3:
            retire(c - 3)
        if c == 0:
            forward_own()
            loop(slots - slots // 2, lambda j: split_corr(slots // 2 + j))
            out[...] = jnp.zeros_like(out)
        if c == 1:
            where_slots()
            judge()
        if c == 3:
            for i in range(depth - 2):
                relay_flag(i)
        if c == 4:
            relay_flag(depth - 2)
            for t in range(1, parts):
                b_arrival(t).wait_recv()
            far(0, 2)
        if c == 5:
            relay_flag(depth - 1)
            share_flag()
            far(2, levels)
    close_flag()
    ready(early)
    loop(slots, lambda j: near(early, j), UNROLL)
    ready(late)
    loop(slots, lambda j: near(late, j), UNROLL)
    for ch in range(steps - 3, steps):
        retire(ch)

    @pl.when(end)
    def _():
        for q in range(4):
            e_copy(q).wait_send()

    for o in (1, 2, 3):
        q_copy(o).wait_send()
    for t in range(1, parts):
        b_copy(t).wait_send()
        side_copy(t).wait_send()
    for d in range(2):
        @pl.when(rank(d) < depth - 1)
        def _(d=d):
            flag_copy(d).wait_send()


def whole_call(depth, parts, density, green_table, corrections, interp_index, interp_frac, pairs, counts):
    peers = 4 * depth
    rhs, dofs = density.shape
    slots, block, _ = corrections.shape
    levels = green_table.shape[0]
    f32, bf16 = jnp.float32, jnp.bfloat16
    vmem = pl.BlockSpec(memory_space=pltpu.VMEM)
    anywhere = pl.BlockSpec(memory_space=pl.ANY)
    held_words = (depth + parts + 2) * rhs * dofs + 6 * depth * rhs * block
    words = held_words + 2 * (slots + levels) * block * block + 5 * peers * block
    dma = pltpu.SemaphoreType.DMA
    return pl.pallas_call(
        functools.partial(kernel, depth, parts),
        out_shape=jax.ShapeDtypeStruct(density.shape, f32),
        in_specs=[anywhere, pl.BlockSpec(memory_space=pltpu.SMEM)] + [anywhere] * 5,
        out_specs=vmem,
        scratch_shapes=[
            pltpu.SMEM(pairs.shape, jnp.int32),
            pltpu.SMEM(interp_index.shape, jnp.int32),
            pltpu.SMEM(interp_frac.shape, f32),
            pltpu.VMEM((depth, rhs, dofs), f32),
            pltpu.VMEM((depth, 3, rhs, block), f32),
            pltpu.VMEM((depth, 3, rhs, block), f32),
            pltpu.VMEM((parts, rhs, dofs), f32),
            pltpu.VMEM((slots, block, block), f32),
            pltpu.VMEM((slots, block, block), bf16),
            pltpu.VMEM((slots, block, block), bf16),
            pltpu.VMEM((levels, block, block), f32),
            pltpu.VMEM((levels, block, block), bf16),
            pltpu.VMEM((levels, block, block), bf16),
            pltpu.VMEM((peers, block), jnp.int32),
            pltpu.VMEM((3, peers, block), jnp.int32),
            pltpu.VMEM((peers, block), jnp.int32),
            pltpu.SMEM((peers,), jnp.int32),
            pltpu.VMEM((dofs // block * rhs, block), f32),
            dma((slots + levels,)),
            dma((5,)),
            dma((2, depth - 1)),
            dma((2, depth - 1, CHUNKS)),
            dma((depth, 3)),
            dma((depth, 3)),
            dma((parts - 1,)),
            dma((parts - 1,)),
            dma((3,)),
            dma((3,)),
        ],
        compiler_params=pltpu.CompilerParams(
            collective_id=0, has_side_effects=True, vmem_limit_bytes=4 * words + 8 * 2**20
        ),
    )(pairs, counts, interp_index, interp_frac, density, green_table, corrections)


def packed_call(depth, parts, density, green_table, corrections, interp_index, interp_frac, pairs, counts):
    rhs, dofs = density.shape
    slots, block, _ = corrections.shape
    levels = green_table.shape[0]
    rows = dofs // block
    f32, bf16, i32 = jnp.float32, jnp.bfloat16, jnp.int32
    anywhere = pl.BlockSpec(memory_space=pl.ANY)
    smem = pl.BlockSpec(memory_space=pltpu.SMEM)
    room = capacity(depth, rows)
    sizes, _ = cuts(rhs)
    steps = len(sizes)
    blocks = depth * rows + 2 * 4 * depth + 4 * depth + room
    words = blocks * rhs * block + 2 * (slots + levels) * block * block + (parts + 2) * rhs * dofs
    dma = pltpu.SemaphoreType.DMA
    line = max(128, 4 * depth)
    return pl.pallas_call(
        functools.partial(packed_kernel, depth, parts, block),
        out_shape=(jax.ShapeDtypeStruct(density.shape, f32), jax.ShapeDtypeStruct((1,), i32)),
        in_specs=[anywhere, smem] + [anywhere] * 5,
        out_specs=(pl.BlockSpec(memory_space=pltpu.VMEM), smem),
        scratch_shapes=[
            pltpu.SMEM(pairs.shape, i32),
            pltpu.SMEM(interp_index.shape, i32),
            pltpu.SMEM(interp_frac.shape, f32),
            pltpu.VMEM((parts, rhs, dofs), f32),
            pltpu.VMEM((slots, block, block), f32),
            pltpu.VMEM((slots, block, block), bf16),
            pltpu.VMEM((slots, block, block), bf16),
            pltpu.VMEM((levels, block, block), f32),
            pltpu.VMEM((levels, block, block), bf16),
            pltpu.VMEM((levels, block, block), bf16),
            pltpu.VMEM((rows * rhs, block), f32),
            pltpu.SMEM((line,), i32),
            pltpu.SMEM((3, line), i32),
            pltpu.SMEM((4, line), i32),
            pltpu.SMEM((depth * rows,), i32),
            pltpu.SMEM((depth * rows,), i32),
            pltpu.SMEM((room,), i32),
            pltpu.SMEM((4 * depth,), i32),
            pltpu.SMEM((4 * (depth - 1),), i32),
            pltpu.SMEM((slots,), i32),
            pltpu.SMEM((slots,), i32),
            pltpu.SMEM((slots,), i32),
            pltpu.SMEM((3, line), i32),
            pltpu.SMEM((line,), i32),
            pltpu.SMEM((line,), i32),
            pltpu.SMEM((parts - 1, line), i32),
            dma((slots + levels,)),
            dma((4,)),
            dma((2, depth, steps)),
            dma((2, depth, steps)),
            dma((3, steps)),
            dma((3, steps)),
            dma((parts - 1,)),
            dma((parts - 1,)),
            dma((3,)),
            dma((3,)),
            dma((4,)),
            dma((4,)),
            dma((4, DIRECT)),
            dma((4, DIRECT)),
            dma((2,)),
            dma((2,)),
            dma((parts - 1,)),
            dma((parts - 1,)),
        ]
        + [pltpu.VMEM((depth * rows, m, block), f32) for m in sizes]
        + [pltpu.VMEM((4 * depth, m, block), f32) for m in sizes]
        + [pltpu.VMEM((4 * depth, m, block), f32) for m in sizes]
        + [pltpu.VMEM((room, m, block), f32) for m in sizes[:-DIRECT]]
        + [pltpu.VMEM((4 * (depth - 1), m, block), f32) for m in sizes[-DIRECT:]],
        compiler_params=pltpu.CompilerParams(
            collective_id=1, has_side_effects=True, vmem_limit_bytes=4 * words + 8 * 2**20
        ),
    )(pairs, counts, interp_index, interp_frac, density, green_table, corrections)


def local(peers, parts, density, green_table, corrections, interp_index, interp_frac, pairs, counts):
    depth = peers // 4
    fix = functools.partial(pltpu.with_memory_space_constraint, memory_space=pltpu.HBM)
    held = (fix(density), fix(green_table), fix(corrections), fix(interp_index), fix(interp_frac), fix(pairs.T), counts)
    if depth < 4:
        return 0.5 * density + whole_call(depth, parts, *held)
    found, spill = packed_call(depth, parts, *held)
    return lax.cond(
        spill[0] > 0,
        lambda: 0.5 * density + whole_call(depth, parts, *held),
        lambda: 0.5 * density + found,
    )


def solution(mesh):
    placed = (
        P(None, ("wide", "blk")),
        P(("wide", "blk"), None, None),
        P(("wide", "blk"), None, None),
        P(("wide", "blk"), None),
        P(("wide", "blk"), None),
        P(("wide", "blk"), None),
        P(("wide", "blk")),
    )
    return jax.shard_map(
        functools.partial(local, mesh.shape["wide"], mesh.shape["blk"]),
        mesh=mesh, in_specs=placed, out_specs=P(None, ("wide", "blk")), check_vma=False,
    )
```

```python
import functools

import jax
import jax.numpy as jnp
from jax import lax
from jax.experimental import pallas as pl
from jax.experimental.pallas import tpu as pltpu
from jax.sharding import PartitionSpec as P

MESH = pl.DeviceIdType.MESH
CHUNKS = 8
NN = (((1,), (0,)), ((), ()))


def split(value):
    high = value.astype(jnp.bfloat16)
    low = (value - high.astype(jnp.float32)).astype(jnp.bfloat16)
    return high, low


def product(value, high_t, low_t):
    rows = value.shape[0]
    high, low = split(value)
    both = lax.dot_general(
        jnp.concatenate([high, low], axis=0), high_t, NN, preferred_element_type=jnp.float32
    )
    rest = lax.dot_general(high, low_t, NN, preferred_element_type=jnp.float32)
    return both[:rows] + both[rows:] + rest


def kernel(
    depth, parts,
    pairs_hbm, counts, index_hbm, frac_hbm, density_hbm, green_hbm, corr_hbm,
    out,
    pairs, index, frac,
    held, fsend, frecv, cycle, corr, corr_high, corr_low, green, green_high, green_low,
    request, asked, row_of, slot_of, mixed,
    load_sem, own_sem, z_send, z_recv, f_send, f_recv, b_send, b_recv, q_send, q_recv,
):
    wide = lax.axis_index("wide")
    blk = lax.axis_index("blk")
    core = lax.rem(wide, 2)
    side = lax.rem(lax.div(wide, 2), 2)
    z = lax.div(wide, 4)
    peers = 4 * depth
    rhs, local = density_hbm.shape
    density = cycle.at[blk]
    slots = corr.shape[0]
    levels = green.shape[0]
    block = corr.shape[1]
    rows = local // block
    step_rows = rhs // CHUNKS

    def place(o):
        at_side = 1 - side if o & 2 else side
        at_core = 1 - core if o & 1 else core
        return at_side * 2 + at_core

    def chunk(ch):
        return pl.ds(pl.multiple_of(ch * step_rows, step_rows), step_rows)

    def corr_load(j):
        return pltpu.make_async_copy(corr_hbm.at[j], corr.at[j], load_sem.at[j])

    def green_load(k):
        return pltpu.make_async_copy(green_hbm.at[k], green.at[k], load_sem.at[slots + k])

    def z_copy(d, s, ch, source=None):
        zz = z - s if d == 0 else z + s
        to = wide + 4 if d == 0 else wide - 4
        return pltpu.make_async_remote_copy(
            src_ref=(held.at[zz] if source is None else source).at[chunk(ch)],
            dst_ref=held.at[zz].at[chunk(ch)],
            send_sem=z_send.at[d, s],
            recv_sem=z_recv.at[d, s, ch],
            device_id={"wide": to},
            device_id_type=MESH,
        )

    def z_whole(d, s):
        zz = z - s if d == 0 else z + s
        return pltpu.make_async_remote_copy(
            src_ref=held.at[zz],
            dst_ref=held.at[zz],
            send_sem=z_send.at[d, s],
            recv_sem=z_recv.at[d, s, 0],
            device_id={"wide": wide},
            device_id_type=MESH,
        )

    def z_arrival(d, s, ch):
        zz = z - 1 - s if d == 0 else z + 1 + s
        return pltpu.make_async_remote_copy(
            src_ref=held.at[zz].at[chunk(ch)],
            dst_ref=held.at[zz].at[chunk(ch)],
            send_sem=z_send.at[d, s],
            recv_sem=z_recv.at[d, s, ch],
            device_id={"wide": wide},
            device_id_type=MESH,
        )

    def f_copy(zz, o, window):
        return pltpu.make_async_remote_copy(
            src_ref=fsend.at[zz, o - 1].at[window],
            dst_ref=frecv.at[zz, o - 1].at[window],
            send_sem=f_send.at[zz, o - 1],
            recv_sem=f_recv.at[zz, o - 1],
            device_id={"wide": z * 4 + place(o)},
            device_id_type=MESH,
        )

    def b_copy(t):
        return pltpu.make_async_remote_copy(
            src_ref=density_hbm,
            dst_ref=cycle.at[blk],
            send_sem=b_send.at[t - 1],
            recv_sem=b_recv.at[t - 1],
            device_id={"blk": lax.rem(blk + t, parts)},
            device_id_type=MESH,
        )

    def b_arrival(t):
        source = lax.rem(blk + parts - t, parts)
        return pltpu.make_async_remote_copy(
            src_ref=density_hbm,
            dst_ref=cycle.at[source],
            send_sem=b_send.at[t - 1],
            recv_sem=b_recv.at[t - 1],
            device_id={"blk": lax.rem(blk + t, parts)},
            device_id_type=MESH,
        )

    def q_copy(o):
        return pltpu.make_async_remote_copy(
            src_ref=request,
            dst_ref=asked.at[o - 1],
            send_sem=q_send.at[o - 1],
            recv_sem=q_recv.at[o - 1],
            device_id={"wide": z * 4 + place(o)},
            device_id_type=MESH,
        )

    def z_source(d, s):
        return z - 1 - s if d == 0 else z + 1 + s

    def z_exists(d, s):
        return z - 1 - s >= 0 if d == 0 else z + 1 + s <= depth - 1

    def z_onward(d):
        return z < depth - 1 if d == 0 else z > 0

    def pick(source, window, wanted):
        want = jnp.broadcast_to(wanted, (wanted.shape[0] * window.size, block))
        got = source[window, 0:block]
        for i in range(1, rows):
            got = jnp.where(want == i, source[window, i * block : (i + 1) * block], got)
        return got

    def forward(source, zz, ch):
        mine = zz * 4 + place(0)
        for o in (2, 3, 1):
            wanted = asked[o - 1, pl.ds(mine, 1), :]
            fsend[zz, o - 1, chunk(ch), :] = pick(source, chunk(ch), wanted)
            f_copy(zz, o, chunk(ch)).start()

    def near_one(value, peer):
        j = slot_of[peer]
        found = product(value, corr_high[j], corr_low[j])
        row = jnp.broadcast_to(row_of[pl.ds(peer, 1), :], (rhs, block))
        for r in range(rows):
            at = slice(r * block, (r + 1) * block)
            out[:, at] += jnp.where(row == r, found, 0.0)

    def near(source, zz):
        mine = zz * 4 + place(0)
        near_one(pick(source, pl.ds(0, rhs), request[pl.ds(mine, 1), :]), mine)
        for o in (1, 2, 3):
            f_copy(zz, o, pl.ds(0, rhs)).wait_recv()
            near_one(frecv[zz, o - 1], zz * 4 + place(o))

    def loop(count, body):
        lax.fori_loop(0, count, lambda i, c: (body(i), c)[1], 0)

    barrier = pltpu.get_barrier_semaphore()
    for d in range(2):
        @pl.when(z_onward(d))
        def _(d=d):
            pl.semaphore_signal(
                barrier, inc=1, device_id={"wide": wide + 4 if d == 0 else wide - 4}, device_id_type=MESH
            )
    for o in (1, 2, 3):
        pl.semaphore_signal(barrier, inc=1, device_id={"wide": z * 4 + place(o)}, device_id_type=MESH)
    for t in range(1, parts):
        pl.semaphore_signal(barrier, inc=1, device_id={"blk": lax.rem(blk + t, parts)}, device_id_type=MESH)

    ends = jnp.where(z < depth - 1, 1, 0) + jnp.where(z > 0, 1, 0)
    pl.semaphore_wait(barrier, 3 + parts - 1 + ends)

    def send_own(ch):
        for d in range(2):
            @pl.when(z_onward(d))
            def _(d=d):
                z_copy(d, 0, ch, density_hbm).start()

    loop(CHUNKS, send_own)
    for t in range(1, parts):
        b_copy(t).start()
    small = [
        pltpu.make_async_copy(source, target, own_sem.at[1 + i])
        for i, (source, target) in enumerate(
            ((pairs_hbm, pairs), (index_hbm, index), (frac_hbm, frac))
        )
    ]
    for copy in small:
        copy.start()
    own = pltpu.make_async_copy(density_hbm, density, own_sem.at[0])
    own.start()
    loop(levels, lambda k: green_load(k).start())
    loop(slots, lambda j: corr_load(j).start())
    for copy in small:
        copy.wait()

    peer_at = lax.broadcasted_iota(jnp.int32, (peers, block), 0)
    wanted = jnp.zeros((peers, block), jnp.int32)
    row = jnp.full((peers, block), -1, jnp.int32)
    used = counts[0]
    for j in range(slots):
        source = pairs[1, j]
        here = peer_at == lax.div(source, rows)
        wanted = jnp.where(here, lax.rem(source, rows), wanted)
        row = jnp.where(here, jnp.where(j < used, pairs[0, j], -1), row)
    request[...] = wanted
    row_of[...] = row

    def find_slot(p):
        found = jnp.int32(0)
        for j in range(slots):
            found = jnp.where(lax.div(pairs[1, j], rows) == p, j, found)
        slot_of[p] = found

    for o in (2, 3, 1):
        q_copy(o).start()
    loop(peers, find_slot)
    own.wait()
    out[...] = 0.5 * cycle[blk]

    for o in (1, 2, 3):
        q_copy(o).wait_recv()
    loop(CHUNKS, lambda ch: forward(density, z, ch))

    def split_green(k):
        green_load(k).wait()
        green_high[k], green_low[k] = split(green[k].T)

    def split_corr(j):
        corr_load(j).wait()
        corr_high[j], corr_low[j] = split(corr[j].T)

    loop(levels, split_green)
    loop(slots, split_corr)

    def far_level(k):
        def mix(r):
            total = jnp.zeros((rhs, block), jnp.float32)

            def add(q, total):
                for i in range(rows):
                    s = q * rows + i
                    low = index[r, s]
                    f = frac[r, s]
                    zero = jnp.float32(0.0)
                    weight = jnp.where(low == k, 1.0 - f, zero) + jnp.where(low + 1 == k, f, zero)
                    total = total + weight * cycle[q, :, i * block : (i + 1) * block]
                return total

            mixed[pl.ds(pl.multiple_of(r * rhs, rhs), rhs), :] = lax.fori_loop(0, parts, add, total)

        loop(rows, mix)
        found = product(mixed[...], green_high[k], green_low[k])
        for r in range(rows):
            out[:, r * block : (r + 1) * block] += found[r * rhs : (r + 1) * rhs]

    def take(s):
        def one(ch):
            for d in range(2):
                @pl.when(z_exists(d, s))
                def _(d=d):
                    z_arrival(d, s, ch).wait_recv()

                    @pl.when(z_onward(d))
                    def _():
                        z_copy(d, s + 1, ch).start()

                    forward(held.at[z_source(d, s)], z_source(d, s), ch)

        loop(CHUNKS, one)

    def near_step(s):
        for d in range(2):
            @pl.when(z_exists(d, s))
            def _(d=d):
                near(held.at[z_source(d, s)], z_source(d, s))

    take(0)
    near(density, z)
    for t in range(1, parts):
        b_arrival(t).wait_recv()
    loop(levels, far_level)

    def later(s):
        take(s)
        near_step(s - 1)

    lax.fori_loop(1, depth - 1, lambda s, c: (later(s), c)[1], 0)
    def z_done(s):
        for d in range(2):
            zz = z - s if d == 0 else z + s
            there = zz >= 0 if d == 0 else zz <= depth - 1

            @pl.when(there)
            def _(d=d):
                @pl.when(z_onward(d))
                def _():
                    z_whole(d, s).wait_send()

    loop(depth - 1, z_done)

    def f_done(zz):
        for o in (1, 2, 3):
            f_copy(zz, o, pl.ds(0, rhs)).wait_send()

    last = jnp.where(z == depth - 1, 0, jnp.where(z == 0, depth - 1, z))

    def f_early(zz):
        @pl.when(zz != last)
        def _():
            f_done(zz)

    loop(depth, f_early)
    for o in (1, 2, 3):
        q_copy(o).wait_send()
    for t in range(1, parts):
        b_copy(t).wait_send()
    near_step(depth - 2)
    f_done(last)


def local(peers, parts, density, green_table, corrections, interp_index, interp_frac, pairs, counts):
    depth = peers // 4
    rhs, dofs = density.shape
    slots, block, _ = corrections.shape
    levels = green_table.shape[0]
    f32, bf16 = jnp.float32, jnp.bfloat16
    vmem = pl.BlockSpec(memory_space=pltpu.VMEM)
    anywhere = pl.BlockSpec(memory_space=pl.ANY)
    held_words = (depth + parts + 2) * rhs * dofs + 6 * depth * rhs * block
    words = held_words + 2 * (slots + levels) * block * block + 5 * peers * block
    dma = pltpu.SemaphoreType.DMA
    fix = functools.partial(pltpu.with_memory_space_constraint, memory_space=pltpu.HBM)
    found = pl.pallas_call(
        functools.partial(kernel, depth, parts),
        out_shape=jax.ShapeDtypeStruct(density.shape, f32),
        in_specs=[anywhere, pl.BlockSpec(memory_space=pltpu.SMEM)] + [anywhere] * 5,
        out_specs=vmem,
        scratch_shapes=[
            pltpu.SMEM(pairs.shape[::-1], jnp.int32),
            pltpu.SMEM(interp_index.shape, jnp.int32),
            pltpu.SMEM(interp_frac.shape, f32),
            pltpu.VMEM((depth, rhs, dofs), f32),
            pltpu.VMEM((depth, 3, rhs, block), f32),
            pltpu.VMEM((depth, 3, rhs, block), f32),
            pltpu.VMEM((parts, rhs, dofs), f32),
            pltpu.VMEM((slots, block, block), f32),
            pltpu.VMEM((slots, block, block), bf16),
            pltpu.VMEM((slots, block, block), bf16),
            pltpu.VMEM((levels, block, block), f32),
            pltpu.VMEM((levels, block, block), bf16),
            pltpu.VMEM((levels, block, block), bf16),
            pltpu.VMEM((peers, block), jnp.int32),
            pltpu.VMEM((3, peers, block), jnp.int32),
            pltpu.VMEM((peers, block), jnp.int32),
            pltpu.SMEM((peers,), jnp.int32),
            pltpu.VMEM((dofs // block * rhs, block), f32),
            dma((slots + levels,)),
            dma((5,)),
            dma((2, depth - 1)),
            dma((2, depth - 1, CHUNKS)),
            dma((depth, 3)),
            dma((depth, 3)),
            dma((parts - 1,)),
            dma((parts - 1,)),
            dma((3,)),
            dma((3,)),
        ],
        compiler_params=pltpu.CompilerParams(
            collective_id=0, has_side_effects=True, vmem_limit_bytes=4 * words + 8 * 2**20
        ),
    )(fix(pairs.T), counts, *(fix(x) for x in (interp_index, interp_frac, density, green_table, corrections)))
    return found


def solution(mesh):
    placed = (
        P(None, ("wide", "blk")),
        P(("wide", "blk"), None, None),
        P(("wide", "blk"), None, None),
        P(("wide", "blk"), None),
        P(("wide", "blk"), None),
        P(("wide", "blk"), None),
        P(("wide", "blk")),
    )
    return jax.shard_map(
        functools.partial(local, mesh.shape["wide"], mesh.shape["blk"]),
        mesh=mesh, in_specs=placed, out_specs=P(None, ("wide", "blk")), check_vma=False,
    )
```

```python
import functools

import jax
import jax.numpy as jnp
from jax import lax
from jax.experimental import pallas as pl
from jax.experimental.pallas import tpu as pltpu
from jax.sharding import PartitionSpec as P

MESH = pl.DeviceIdType.MESH
CHUNKS = 8
NN = (((1,), (0,)), ((), ()))


def split(value):
    high = value.astype(jnp.bfloat16)
    low = (value - high.astype(jnp.float32)).astype(jnp.bfloat16)
    return high, low


def product(value, high_t, low_t):
    rows = value.shape[0]
    high, low = split(value)
    both = lax.dot_general(
        jnp.concatenate([high, low], axis=0), high_t, NN, preferred_element_type=jnp.float32
    )
    rest = lax.dot_general(high, low_t, NN, preferred_element_type=jnp.float32)
    return both[:rows] + both[rows:] + rest


def kernel(
    depth, parts,
    pairs_hbm, counts, index_hbm, frac_hbm, density_hbm, green_hbm, corr_hbm,
    out,
    pairs, index, frac,
    held, fsend, frecv, cycle, corr, corr_high, corr_low, green, green_high, green_low,
    request, asked, row_of, slot_of, mixed,
    load_sem, own_sem, z_send, z_recv, f_send, f_recv, b_send, b_recv, q_send, q_recv,
):
    wide = lax.axis_index("wide")
    blk = lax.axis_index("blk")
    core = lax.rem(wide, 2)
    side = lax.rem(lax.div(wide, 2), 2)
    z = lax.div(wide, 4)
    peers = 4 * depth
    rhs, local = density_hbm.shape
    density = cycle.at[blk]
    slots = corr.shape[0]
    levels = green.shape[0]
    block = corr.shape[1]
    rows = local // block
    step_rows = rhs // CHUNKS

    def place(o):
        at_side = 1 - side if o & 2 else side
        at_core = 1 - core if o & 1 else core
        return at_side * 2 + at_core

    def chunk(ch):
        return pl.ds(pl.multiple_of(ch * step_rows, step_rows), step_rows)

    def corr_load(j):
        return pltpu.make_async_copy(corr_hbm.at[j], corr.at[j], load_sem.at[j])

    def green_load(k):
        return pltpu.make_async_copy(green_hbm.at[k], green.at[k], load_sem.at[slots + k])

    def z_copy(d, s, ch, source=None):
        zz = z - s if d == 0 else z + s
        to = wide + 4 if d == 0 else wide - 4
        return pltpu.make_async_remote_copy(
            src_ref=(held.at[zz] if source is None else source).at[chunk(ch)],
            dst_ref=held.at[zz].at[chunk(ch)],
            send_sem=z_send.at[d, s],
            recv_sem=z_recv.at[d, s, ch],
            device_id={"wide": to},
            device_id_type=MESH,
        )

    def z_whole(d, s):
        zz = z - s if d == 0 else z + s
        return pltpu.make_async_remote_copy(
            src_ref=held.at[zz],
            dst_ref=held.at[zz],
            send_sem=z_send.at[d, s],
            recv_sem=z_recv.at[d, s, 0],
            device_id={"wide": wide},
            device_id_type=MESH,
        )

    def z_arrival(d, s, ch):
        zz = z - 1 - s if d == 0 else z + 1 + s
        return pltpu.make_async_remote_copy(
            src_ref=held.at[zz].at[chunk(ch)],
            dst_ref=held.at[zz].at[chunk(ch)],
            send_sem=z_send.at[d, s],
            recv_sem=z_recv.at[d, s, ch],
            device_id={"wide": wide},
            device_id_type=MESH,
        )

    def f_copy(zz, o, window):
        return pltpu.make_async_remote_copy(
            src_ref=fsend.at[zz, o - 1].at[window],
            dst_ref=frecv.at[zz, o - 1].at[window],
            send_sem=f_send.at[zz, o - 1],
            recv_sem=f_recv.at[zz, o - 1],
            device_id={"wide": z * 4 + place(o)},
            device_id_type=MESH,
        )

    def b_copy(t):
        return pltpu.make_async_remote_copy(
            src_ref=density_hbm,
            dst_ref=cycle.at[blk],
            send_sem=b_send.at[t - 1],
            recv_sem=b_recv.at[t - 1],
            device_id={"blk": lax.rem(blk + t, parts)},
            device_id_type=MESH,
        )

    def b_arrival(t):
        source = lax.rem(blk + parts - t, parts)
        return pltpu.make_async_remote_copy(
            src_ref=density_hbm,
            dst_ref=cycle.at[source],
            send_sem=b_send.at[t - 1],
            recv_sem=b_recv.at[t - 1],
            device_id={"blk": lax.rem(blk + t, parts)},
            device_id_type=MESH,
        )

    def q_copy(o):
        return pltpu.make_async_remote_copy(
            src_ref=request,
            dst_ref=asked.at[o - 1],
            send_sem=q_send.at[o - 1],
            recv_sem=q_recv.at[o - 1],
            device_id={"wide": z * 4 + place(o)},
            device_id_type=MESH,
        )

    def z_source(d, s):
        return z - 1 - s if d == 0 else z + 1 + s

    def z_exists(d, s):
        return z - 1 - s >= 0 if d == 0 else z + 1 + s <= depth - 1

    def z_onward(d):
        return z < depth - 1 if d == 0 else z > 0

    def pick(source, window, wanted):
        want = jnp.broadcast_to(wanted, (wanted.shape[0] * window.size, block))
        got = source[window, 0:block]
        for i in range(1, rows):
            got = jnp.where(want == i, source[window, i * block : (i + 1) * block], got)
        return got

    def forward(source, zz, ch):
        mine = zz * 4 + place(0)
        for o in (2, 3, 1):
            wanted = asked[o - 1, pl.ds(mine, 1), :]
            fsend[zz, o - 1, chunk(ch), :] = pick(source, chunk(ch), wanted)
            f_copy(zz, o, chunk(ch)).start()

    def near_one(value, peer):
        j = slot_of[peer]
        found = product(value, corr_high[j], corr_low[j])
        row = jnp.broadcast_to(row_of[pl.ds(peer, 1), :], (rhs, block))
        for r in range(rows):
            at = slice(r * block, (r + 1) * block)
            out[:, at] += jnp.where(row == r, found, 0.0)

    def near_two(zz):
        peer = [zz * 4 + place(o) for o in (2, 3)]
        slot = [slot_of[p] for p in peer]
        found = [product(frecv[zz, 1 + i], corr_high[slot[i]], corr_low[slot[i]]) for i in range(2)]
        row = [jnp.broadcast_to(row_of[pl.ds(p, 1), :], (rhs, block)) for p in peer]
        for r in range(rows):
            at = slice(r * block, (r + 1) * block)
            both = jnp.where(row[0] == r, found[0], 0.0) + jnp.where(row[1] == r, found[1], 0.0)
            out[:, at] += both

    def near(source, zz):
        mine = zz * 4 + place(0)
        near_one(pick(source, pl.ds(0, rhs), request[pl.ds(mine, 1), :]), mine)
        f_copy(zz, 1, pl.ds(0, rhs)).wait_recv()
        near_one(frecv[zz, 0], zz * 4 + place(1))
        for o in (2, 3):
            f_copy(zz, o, pl.ds(0, rhs)).wait_recv()
        near_two(zz)

    def loop(count, body):
        lax.fori_loop(0, count, lambda i, c: (body(i), c)[1], 0)

    barrier = pltpu.get_barrier_semaphore()
    for d in range(2):
        @pl.when(z_onward(d))
        def _(d=d):
            pl.semaphore_signal(
                barrier, inc=1, device_id={"wide": wide + 4 if d == 0 else wide - 4}, device_id_type=MESH
            )
    for o in (1, 2, 3):
        pl.semaphore_signal(barrier, inc=1, device_id={"wide": z * 4 + place(o)}, device_id_type=MESH)
    for t in range(1, parts):
        pl.semaphore_signal(barrier, inc=1, device_id={"blk": lax.rem(blk + t, parts)}, device_id_type=MESH)

    ends = jnp.where(z < depth - 1, 1, 0) + jnp.where(z > 0, 1, 0)
    pl.semaphore_wait(barrier, 3 + parts - 1 + ends)

    def send_own(ch):
        for d in range(2):
            @pl.when(z_onward(d))
            def _(d=d):
                z_copy(d, 0, ch, density_hbm).start()

    loop(CHUNKS, send_own)
    for t in range(1, parts):
        b_copy(t).start()
    small = [
        pltpu.make_async_copy(source, target, own_sem.at[1 + i])
        for i, (source, target) in enumerate(
            ((pairs_hbm, pairs), (index_hbm, index), (frac_hbm, frac))
        )
    ]
    for copy in small:
        copy.start()
    own = pltpu.make_async_copy(density_hbm, density, own_sem.at[0])
    own.start()
    loop(levels, lambda k: green_load(k).start())
    loop(slots, lambda j: corr_load(j).start())
    for copy in small:
        copy.wait()

    peer_at = lax.broadcasted_iota(jnp.int32, (peers, block), 0)
    wanted = jnp.zeros((peers, block), jnp.int32)
    row = jnp.full((peers, block), -1, jnp.int32)
    used = counts[0]
    for j in range(slots):
        source = pairs[1, j]
        here = peer_at == lax.div(source, rows)
        wanted = jnp.where(here, lax.rem(source, rows), wanted)
        row = jnp.where(here, jnp.where(j < used, pairs[0, j], -1), row)
    request[...] = wanted
    row_of[...] = row

    def find_slot(p):
        found = jnp.int32(0)
        for j in range(slots):
            found = jnp.where(lax.div(pairs[1, j], rows) == p, j, found)
        slot_of[p] = found

    for o in (2, 3, 1):
        q_copy(o).start()
    loop(peers, find_slot)
    own.wait()
    out[...] = 0.5 * cycle[blk]

    for o in (1, 2, 3):
        q_copy(o).wait_recv()
    loop(CHUNKS, lambda ch: forward(density, z, ch))

    def split_green(k):
        green_load(k).wait()
        green_high[k], green_low[k] = split(green[k].T)

    def split_corr(j):
        corr_load(j).wait()
        corr_high[j], corr_low[j] = split(corr[j].T)

    loop(levels, split_green)
    loop(slots, split_corr)

    def far_level(k):
        def mix(r):
            total = jnp.zeros((rhs, block), jnp.float32)

            def add(q, total):
                for i in range(rows):
                    s = q * rows + i
                    low = index[r, s]
                    f = frac[r, s]
                    zero = jnp.float32(0.0)
                    weight = jnp.where(low == k, 1.0 - f, zero) + jnp.where(low + 1 == k, f, zero)
                    total = total + weight * cycle[q, :, i * block : (i + 1) * block]
                return total

            mixed[pl.ds(pl.multiple_of(r * rhs, rhs), rhs), :] = lax.fori_loop(0, parts, add, total)

        loop(rows, mix)
        found = product(mixed[...], green_high[k], green_low[k])
        for r in range(rows):
            out[:, r * block : (r + 1) * block] += found[r * rhs : (r + 1) * rhs]

    def take(s):
        def one(ch):
            for d in range(2):
                @pl.when(z_exists(d, s))
                def _(d=d):
                    z_arrival(d, s, ch).wait_recv()

                    @pl.when(z_onward(d))
                    def _():
                        z_copy(d, s + 1, ch).start()

                    forward(held.at[z_source(d, s)], z_source(d, s), ch)

        loop(CHUNKS, one)

    def near_step(s):
        for d in range(2):
            @pl.when(z_exists(d, s))
            def _(d=d):
                near(held.at[z_source(d, s)], z_source(d, s))

    take(0)
    near(density, z)
    for t in range(1, parts):
        b_arrival(t).wait_recv()
    loop(levels, far_level)

    def later(s):
        take(s)
        near_step(s - 1)

    lax.fori_loop(1, depth - 1, lambda s, c: (later(s), c)[1], 0)
    def z_done(s):
        for d in range(2):
            zz = z - s if d == 0 else z + s
            there = zz >= 0 if d == 0 else zz <= depth - 1

            @pl.when(there)
            def _(d=d):
                @pl.when(z_onward(d))
                def _():
                    z_whole(d, s).wait_send()

    loop(depth - 1, z_done)

    def f_done(zz):
        for o in (1, 2, 3):
            f_copy(zz, o, pl.ds(0, rhs)).wait_send()

    last = jnp.where(z == depth - 1, 0, jnp.where(z == 0, depth - 1, z))

    def f_early(zz):
        @pl.when(zz != last)
        def _():
            f_done(zz)

    loop(depth, f_early)
    for o in (1, 2, 3):
        q_copy(o).wait_send()
    for t in range(1, parts):
        b_copy(t).wait_send()
    near_step(depth - 2)
    f_done(last)


def local(peers, parts, density, green_table, corrections, interp_index, interp_frac, pairs, counts):
    depth = peers // 4
    rhs, dofs = density.shape
    slots, block, _ = corrections.shape
    levels = green_table.shape[0]
    f32, bf16 = jnp.float32, jnp.bfloat16
    vmem = pl.BlockSpec(memory_space=pltpu.VMEM)
    anywhere = pl.BlockSpec(memory_space=pl.ANY)
    held_words = (depth + parts + 2) * rhs * dofs + 6 * depth * rhs * block
    words = held_words + 2 * (slots + levels) * block * block + 5 * peers * block
    dma = pltpu.SemaphoreType.DMA
    fix = functools.partial(pltpu.with_memory_space_constraint, memory_space=pltpu.HBM)
    found = pl.pallas_call(
        functools.partial(kernel, depth, parts),
        out_shape=jax.ShapeDtypeStruct(density.shape, f32),
        in_specs=[anywhere, pl.BlockSpec(memory_space=pltpu.SMEM)] + [anywhere] * 5,
        out_specs=vmem,
        scratch_shapes=[
            pltpu.SMEM(pairs.shape[::-1], jnp.int32),
            pltpu.SMEM(interp_index.shape, jnp.int32),
            pltpu.SMEM(interp_frac.shape, f32),
            pltpu.VMEM((depth, rhs, dofs), f32),
            pltpu.VMEM((depth, 3, rhs, block), f32),
            pltpu.VMEM((depth, 3, rhs, block), f32),
            pltpu.VMEM((parts, rhs, dofs), f32),
            pltpu.VMEM((slots, block, block), f32),
            pltpu.VMEM((slots, block, block), bf16),
            pltpu.VMEM((slots, block, block), bf16),
            pltpu.VMEM((levels, block, block), f32),
            pltpu.VMEM((levels, block, block), bf16),
            pltpu.VMEM((levels, block, block), bf16),
            pltpu.VMEM((peers, block), jnp.int32),
            pltpu.VMEM((3, peers, block), jnp.int32),
            pltpu.VMEM((peers, block), jnp.int32),
            pltpu.SMEM((peers,), jnp.int32),
            pltpu.VMEM((dofs // block * rhs, block), f32),
            dma((slots + levels,)),
            dma((5,)),
            dma((2, depth - 1)),
            dma((2, depth - 1, CHUNKS)),
            dma((depth, 3)),
            dma((depth, 3)),
            dma((parts - 1,)),
            dma((parts - 1,)),
            dma((3,)),
            dma((3,)),
        ],
        compiler_params=pltpu.CompilerParams(
            collective_id=0, has_side_effects=True, vmem_limit_bytes=4 * words + 8 * 2**20
        ),
    )(fix(pairs.T), counts, *(fix(x) for x in (interp_index, interp_frac, density, green_table, corrections)))
    return found


def solution(mesh):
    placed = (
        P(None, ("wide", "blk")),
        P(("wide", "blk"), None, None),
        P(("wide", "blk"), None, None),
        P(("wide", "blk"), None),
        P(("wide", "blk"), None),
        P(("wide", "blk"), None),
        P(("wide", "blk")),
    )
    return jax.shard_map(
        functools.partial(local, mesh.shape["wide"], mesh.shape["blk"]),
        mesh=mesh, in_specs=placed, out_specs=P(None, ("wide", "blk")), check_vma=False,
    )
```
